32 devices in a mesh: wide: 8 (over z, y), fields: 4 (over x, core).
Axes of the slice: x: 2, y: 2, z: 4, core: 2. Of those that a mesh axis runs over, the one named last changes fastest.
Arguments:
- vectors: float32 [256, 16384], P('wide', 'fields'), may hold values from 0.03 to 82, as said below
- pivot_ids: int32 [8], replicated, may hold values from 0 to 255
Outputs:
- similarity: float32 [256, 4, 256], P('wide', None, 'fields')
The draws below stay inside these ranges and needn't reach their ends.
Inputs may be any that keep to these rules, and one draw needn't show every extreme that they name: `vectors`: every entry is positive.
All inputs are finite; a program needn't handle non-finite values.
Results may differ from the reference program's by a relative error of at most 0.0003.
Values sent between devices are 32-bit elements; how exact they have to be, the bound alone decides.
A program may use at most 64 MiB of HBM per device.

```python
import math
import jax
import jax.numpy as jnp
from jax import lax

F = 16384
VB = 32
P_SIZE = 8
STEPS = 4
NVEC = 256
N_WIDE = 8


def draw_vectors(key, part):
    first, second, third = jax.random.split(jax.random.fold_in(key, 11), 3)
    base = jnp.exp(jax.random.uniform(first, (NVEC, F), jnp.float32, -1.0, 1.0))
    row_scale = jnp.exp(jax.random.uniform(second, (NVEC, 1), jnp.float32, 0.0, math.log(10.0)))
    column_scale = jnp.exp(jax.random.uniform(third, (1, F), jnp.float32, math.log(0.3), math.log(3.0)))
    return (base * row_scale * column_scale).astype(jnp.float32)


def set_ends(drawn, key, low, largest):
    index_at = [jax.random.randint(jax.random.fold_in(key, axis), (), 0, length) for axis, length in enumerate(drawn.shape)]
    main_axis = drawn.shape.index(max(drawn.shape))
    beside = index_at[:main_axis] + [(index_at[main_axis] + 1) % drawn.shape[main_axis]] + index_at[main_axis + 1:]
    return drawn.at[tuple(index_at)].set(low).at[tuple(beside)].set(largest)


def setup_inputs(seed: int = 0) -> dict:
    key_list = jax.random.split(jax.random.key(seed), 3)
    vectors = draw_vectors(jax.random.fold_in(key_list[2], 71), 0)
    pivot_ids = set_ends(jax.random.randint(key_list[1], (P_SIZE,), 0, NVEC), jax.random.fold_in(key_list[1], 1), 0, NVEC - 1).astype(jnp.int32)
    return dict(vectors=vectors, pivot_ids=pivot_ids)


def triple_table(owned, pivots, minima, partner):
    with_pivot = jnp.sum(minima, axis=-1)
    pivot_side = jnp.sum(jnp.minimum(pivots[:, None, :], partner[None, :, :]), axis=-1)
    pair_side = jnp.sum(jnp.minimum(owned[:, None, :], partner[None, :, :]), axis=-1)
    triple = lax.map(lambda layer: jnp.sum(jnp.minimum(layer[:, None, :], partner[None, :, :]), axis=-1), jnp.transpose(minima, (1, 0, 2)))
    return with_pivot[:, :, None] + pivot_side[None, :, :] + pair_side[:, None, :] - jnp.transpose(triple, (1, 0, 2))


def reference(vectors, pivot_ids):
    totals = jnp.sum(vectors, axis=1)
    pivots = jnp.take(vectors, pivot_ids, axis=0)
    pivot_totals = jnp.take(totals, pivot_ids, axis=0)
    blocks = vectors.reshape(N_WIDE, VB, F)
    block_totals = totals.reshape(N_WIDE, VB)

    def one_block(block_index):
        owned = blocks[block_index]
        owned_total = block_totals[block_index]
        minima = jnp.minimum(owned[:, None, :], pivots[None, :, :])
        step_rows = []
        for stride in range(1, STEPS + 1):
            source = (block_index - stride) % N_WIDE
            partner = blocks[source]
            partner_total = block_totals[source]
            numerator = triple_table(owned, pivots, minima, partner)
            denominator = owned_total[:, None, None] + pivot_totals[None, :, None] + partner_total[None, None, :]
            step_rows.append((1.5 * numerator / denominator).reshape(VB, P_SIZE * VB))
        return jnp.stack(step_rows, axis=1)

    table = lax.map(one_block, jnp.arange(N_WIDE, dtype=jnp.int32))
    return table.reshape(NVEC, STEPS, P_SIZE * VB)
```

```python
import functools

import jax
import jax.numpy as jnp
from jax import lax
from jax.experimental import pallas as pl
from jax.experimental.pallas import tpu as pltpu
from jax.sharding import PartitionSpec as P

STEPS = 4
LANES = 128
SUB = 8
MESH = pl.DeviceIdType.MESH


def from_behind(value, axis, steps):
    count = lax.axis_size(axis)
    pairs = [(source, (source + steps) % count) for source in range(count)]
    return lax.ppermute(value, axis, pairs)


def plain_body(vectors, pivot_ids):
    row_count = vectors.shape[0]
    pivot_count = pivot_ids.shape[0]
    first_row = lax.axis_index("wide") * row_count
    chosen = (
        pivot_ids[:, None] == first_row + jnp.arange(row_count, dtype=jnp.int32)[None, :]
    ).astype(jnp.float32)
    pivot_part = jnp.dot(
        chosen, vectors, precision=lax.Precision.HIGHEST, preferred_element_type=jnp.float32
    )
    pivots = lax.psum(pivot_part, "wide")
    owned_total, pivot_total = lax.psum(
        (jnp.sum(vectors, axis=1), jnp.sum(pivots, axis=1)), "fields"
    )
    low = jnp.minimum(vectors[:, None, :], pivots[None, :, :])
    high = jnp.maximum(vectors[:, None, :], pivots[None, :, :])
    low_sum = jnp.sum(low, axis=-1)
    partner, partner_total = (vectors, owned_total)
    numerators = []
    partner_totals = []
    for stride in range(1, STEPS + 1):
        partner, partner_total = from_behind((partner, partner_total), "wide", 1)
        partner_totals.append(partner_total)
        rest = lax.map(
            lambda layer: jnp.sum(jnp.minimum(layer[:, None, :], partner[None, :, :]), axis=-1),
            jnp.transpose(high, (1, 0, 2)),
        )
        numerator = low_sum[:, :, None] + jnp.transpose(rest, (1, 0, 2))
        numerators.append(numerator.reshape(row_count, pivot_count * row_count))
    stacked = jnp.stack(numerators, axis=1)
    shares = lax.psum_scatter(stacked, "fields", scatter_dimension=2, tiled=True)
    share_width = shares.shape[2]
    offset = lax.axis_index("fields") * share_width
    step_totals = jnp.stack(partner_totals, axis=0)
    denominator = (
        owned_total[:, None, None, None]
        + pivot_total[None, None, :, None]
        + step_totals[None, :, None, :]
    )
    denominator = denominator.reshape(row_count, STEPS, pivot_count * row_count)
    denominator = lax.dynamic_slice_in_dim(denominator, offset, share_width, 2)
    return 1.5 * shares / denominator


def kernel(n_wide, n_fields, ids_ref, v_ref, out_ref, part, contrib, given, piv, pb, acc, low,
           own_sum, part_sum, msg, got, load_sem, c_send, c_recv, p_send, p_recv, b_send, b_recv,
           r_send, r_recv):
    rows = v_ref.shape[0]
    pivots = piv.shape[1]
    width = part.shape[3]
    cols = width // LANES
    share = pivots // n_fields
    me = lax.axis_index("wide")
    field = lax.axis_index("fields")
    parity = lax.rem(me, 2)
    beside = me + 1 - 2 * parity
    ahead = lax.rem(me + 2, n_wide)

    def wide_peer(d):
        return {"wide": lax.rem(me + d, n_wide)}

    def field_peer(d):
        return {"fields": lax.rem(field + d, n_fields)}

    for i in range(n_wide):
        pltpu.make_async_copy(
            v_ref.at[:, pl.ds(i * width, width)], part.at[i, 0], load_sem.at[i]
        ).start()

    barrier = pltpu.get_barrier_semaphore()
    for d in range(1, n_wide):
        pl.semaphore_signal(barrier, inc=1, device_id=wide_peer(d), device_id_type=MESH)
    for d in range(1, n_fields):
        pl.semaphore_signal(barrier, inc=1, device_id=field_peer(d), device_id_type=MESH)

    for q in range(pivots):
        row = ids_ref[q] - me * rows
        inside = jnp.logical_and(row >= 0, row < rows)
        values = v_ref[pl.ds(jnp.where(inside, row, 0), 1), :]
        values = jnp.where(inside, values, 0.0)
        for i in range(n_wide):
            contrib[i, q : q + 1, :] = values[:, i * width : (i + 1) * width]
    for i in range(n_wide):
        pltpu.make_async_copy(
            v_ref.at[:, pl.ds(i * width, width)], part.at[i, 0], load_sem.at[i]
        ).wait()
    pl.semaphore_wait(barrier, n_wide - 1 + n_fields - 1)

    def c_copy(d):
        return pltpu.make_async_remote_copy(
            src_ref=contrib.at[lax.rem(me + d, n_wide)], dst_ref=given.at[d],
            send_sem=c_send.at[d], recv_sem=c_recv.at[d],
            device_id=wide_peer(d), device_id_type=MESH)

    def p_copy(d):
        return pltpu.make_async_remote_copy(
            src_ref=piv.at[me], dst_ref=piv.at[me],
            send_sem=p_send.at[d], recv_sem=p_recv.at[d],
            device_id=wide_peer(d), device_id_type=MESH)

    def b_copy(kind, i, source, slot, target):
        return pltpu.make_async_remote_copy(
            src_ref=part.at[i, source], dst_ref=part.at[i, slot],
            send_sem=b_send.at[kind, i], recv_sem=b_recv.at[kind, i],
            device_id={"wide": target}, device_id_type=MESH)

    def hop_ahead(i):
        return b_copy(0, i, 0, 2, ahead)

    def relay_ahead(i):
        return b_copy(1, i, 2, 4, ahead)

    def first_beside(i):
        return b_copy(2, i, 2 * parity, 1, beside)

    def second_beside(i):
        return b_copy(3, i, 2 + 2 * parity, 3, beside)

    def stage0(i):
        hop_ahead(i).start()

        @pl.when(parity == 0)
        def _():
            first_beside(i).start()

    def stage1(i):
        hop_ahead(i).wait_recv()
        relay_ahead(i).start()

        @pl.when(parity == 1)
        def _():
            first_beside(i).start()

        @pl.when(parity == 0)
        def _():
            second_beside(i).start()

    def stage2(i):
        relay_ahead(i).wait_recv()

        @pl.when(parity == 1)
        def _():
            second_beside(i).start()

    for d in range(1, n_wide):
        c_copy(d).start()
    stage0(0)
    stage0(1)
    acc[...] = jnp.zeros_like(acc)
    low[...] = jnp.zeros_like(low)
    own_sum[...] = jnp.zeros_like(own_sum)
    part_sum[...] = jnp.zeros_like(part_sum)
    for d in range(1, n_wide):
        c_copy(d).wait_recv()
    total = contrib[me]
    for d in range(1, n_wide):
        total = total + given[d]
    piv[me] = total
    for d in range(1, n_wide):
        p_copy(d).start()
    stage1(0)
    stage0(2)
    stage1(1)
    stage2(0)
    for d in range(1, n_wide):
        source = lax.rem(me + n_wide - d, n_wide)
        pltpu.make_async_remote_copy(
            src_ref=piv.at[source], dst_ref=piv.at[source],
            send_sem=p_send.at[d], recv_sem=p_recv.at[d],
            device_id=wide_peer(d), device_id_type=MESH).wait_recv()

    groups = rows // SUB

    def step(i, carry):
        @pl.when(i + 3 < n_wide)
        def _():
            stage0(i + 3)

        @pl.when(i + 2 < n_wide)
        def _():
            stage1(i + 2)

        @pl.when(i + 1 < n_wide)
        def _():
            stage2(i + 1)

        first_beside(i).wait_recv()
        second_beside(i).wait_recv()

        pb[...] = jnp.broadcast_to(piv[i][:, None, :], pb.shape)
        for k in range(cols):
            lane = slice(k * LANES, (k + 1) * LANES)
            own_sum[...] += part[i, 0, :, lane]
            for s in range(STEPS):
                part_sum[s] += part[i, s + 1, :, lane]

        def per_row(v, inner):
            high = []
            low_now = None
            own = v_ref[pl.ds(v, 1), pl.ds(pl.multiple_of(i * width, LANES), width)]
            for k in range(cols):
                lane = slice(k * LANES, (k + 1) * LANES)
                mine = jnp.broadcast_to(own[:, lane], (SUB, LANES))
                high.append(jnp.maximum(mine[None], pb[:, :, lane]))
                small = jnp.minimum(mine, piv[i, :, lane])
                low_now = small if low_now is None else low_now + small
            low[v] += low_now
            for s in range(STEPS):
                for g in range(groups):
                    sums = None
                    for k in range(cols):
                        lane = slice(k * LANES, (k + 1) * LANES)
                        other = part[i, s + 1, g * SUB : (g + 1) * SUB, lane]
                        term = jnp.minimum(high[k], other[None])
                        sums = term if sums is None else sums + term
                    at = s * rows + g * SUB
                    acc[v, :, at : at + SUB, :] += sums
            return inner

        lax.fori_loop(0, rows, per_row, 0)
        return carry

    lax.fori_loop(0, n_wide, step, 0)

    def finish(v, inner):
        low_sum = jnp.sum(low[v], axis=-1, keepdims=True)
        for q in range(pivots):
            line = jnp.sum(acc[v, q].T, axis=0, keepdims=True) + low_sum[q : q + 1]
            msg[q // share, pl.ds(q % share * rows + v, 1), :] = line
        return inner

    lax.fori_loop(0, rows, finish, 0)
    own_total = jnp.sum(own_sum[...], axis=-1, keepdims=True)
    part_total = jnp.sum(part_sum[...].reshape(STEPS * rows, LANES).T, axis=0, keepdims=True)
    pivot_total = jnp.sum(jnp.sum(piv[...], axis=0), axis=-1, keepdims=True)
    pivot_total = jnp.broadcast_to(pivot_total, (pivots, LANES))
    base = own_total + part_total
    for j in range(n_fields):
        msg[j, share * rows : (share + 1) * rows, :] = base
        at = (share + 1) * rows
        for q in range(pivots):
            turned = (j * share + q) % pivots
            msg[j, at + q : at + q + 1, :] = pivot_total[turned : turned + 1]

    def r_copy(d):
        return pltpu.make_async_remote_copy(
            src_ref=msg.at[lax.rem(field + d, n_fields)], dst_ref=got.at[d],
            send_sem=r_send.at[d], recv_sem=r_recv.at[d],
            device_id=field_peer(d), device_id_type=MESH)

    for d in range(1, n_fields):
        r_copy(d).start()
    for d in range(1, n_fields):
        r_copy(d).wait_recv()
    whole = msg[field]
    for d in range(1, n_fields):
        whole = whole + got[d]
    base = whole[share * rows : (share + 1) * rows]
    at = (share + 1) * rows
    for q in range(share):
        denominator = base + whole[at + q : at + q + 1]
        out_ref[q] = 1.5 * whole[q * rows : (q + 1) * rows] / denominator

    for d in range(1, n_wide):
        c_copy(d).wait_send()
        p_copy(d).wait_send()
    for i in range(n_wide):
        hop_ahead(i).wait_send()
        relay_ahead(i).wait_send()
        first_beside(i).wait_send()
        second_beside(i).wait_send()
    for d in range(1, n_fields):
        r_copy(d).wait_send()


def fused_body(vectors, pivot_ids, n_wide, n_fields):
    rows, local = vectors.shape
    pivots = pivot_ids.shape[0]
    width = local // n_wide
    share = pivots // n_fields
    f32 = jnp.float32
    dma = pltpu.SemaphoreType.DMA
    lines = (share + 1) * rows + pivots
    table = pl.pallas_call(
        functools.partial(kernel, n_wide, n_fields),
        out_shape=jax.ShapeDtypeStruct((share, rows, STEPS * rows), f32),
        in_specs=[
            pl.BlockSpec(memory_space=pltpu.SMEM),
            pl.BlockSpec(memory_space=pltpu.VMEM),
        ],
        out_specs=pl.BlockSpec(memory_space=pltpu.VMEM),
        scratch_shapes=[
            pltpu.VMEM((n_wide, STEPS + 1, rows, width), f32),
            pltpu.VMEM((n_wide, pivots, width), f32),
            pltpu.VMEM((n_wide, pivots, width), f32),
            pltpu.VMEM((n_wide, pivots, width), f32),
            pltpu.VMEM((pivots, SUB, width), f32),
            pltpu.VMEM((rows, pivots, STEPS * rows, LANES), f32),
            pltpu.VMEM((rows, pivots, LANES), f32),
            pltpu.VMEM((rows, LANES), f32),
            pltpu.VMEM((STEPS, rows, LANES), f32),
            pltpu.VMEM((n_fields, lines, LANES), f32),
            pltpu.VMEM((n_fields, lines, LANES), f32),
            dma((n_wide,)),
            dma((n_wide,)), dma((n_wide,)),
            dma((n_wide,)), dma((n_wide,)),
            dma((4, n_wide)), dma((4, n_wide)),
            dma((n_fields,)), dma((n_fields,)),
        ],
        compiler_params=pltpu.CompilerParams(
            collective_id=0, has_side_effects=True, vmem_limit_bytes=48 * 1024 * 1024
        ),
    )(pivot_ids, vectors)
    table = table.reshape(share, rows, STEPS, rows)
    return jnp.transpose(table, (1, 2, 0, 3)).reshape(rows, STEPS, share * rows)


def solution(mesh):
    n_wide = mesh.shape["wide"]
    n_fields = mesh.shape["fields"]

    def body(vectors, pivot_ids):
        rows, local = vectors.shape
        pivots = pivot_ids.shape[0]
        fits = (
            n_wide % 2 == 0 and n_wide > STEPS and local % (n_wide * LANES) == 0
            and pivots % n_fields == 0 and pivots == SUB and rows % SUB == 0
            and STEPS * rows == LANES
        )
        if fits:
            return fused_body(vectors, pivot_ids, n_wide, n_fields)
        return plain_body(vectors, pivot_ids)

    placed = (P("wide", "fields"), P())
    return jax.shard_map(
        body, mesh=mesh, in_specs=placed, out_specs=P("wide", None, "fields"), check_vma=False
    )
```

```python
import functools

import jax
import jax.numpy as jnp
from jax import lax
from jax.experimental import pallas as pl
from jax.experimental.pallas import tpu as pltpu
from jax.sharding import PartitionSpec as P

STEPS = 4
LANES = 128
SUB = 8
PACK = 16
QGROUP = 4
MESH = pl.DeviceIdType.MESH


def from_behind(value, axis, steps):
    count = lax.axis_size(axis)
    pairs = [(source, (source + steps) % count) for source in range(count)]
    return lax.ppermute(value, axis, pairs)


def plain_body(vectors, pivot_ids):
    row_count = vectors.shape[0]
    pivot_count = pivot_ids.shape[0]
    first_row = lax.axis_index("wide") * row_count
    chosen = (
        pivot_ids[:, None] == first_row + jnp.arange(row_count, dtype=jnp.int32)[None, :]
    ).astype(jnp.float32)
    pivot_part = jnp.dot(
        chosen, vectors, precision=lax.Precision.HIGHEST, preferred_element_type=jnp.float32
    )
    pivots = lax.psum(pivot_part, "wide")
    owned_total, pivot_total = lax.psum(
        (jnp.sum(vectors, axis=1), jnp.sum(pivots, axis=1)), "fields"
    )
    low = jnp.minimum(vectors[:, None, :], pivots[None, :, :])
    high = jnp.maximum(vectors[:, None, :], pivots[None, :, :])
    low_sum = jnp.sum(low, axis=-1)
    partner, partner_total = (vectors, owned_total)
    numerators = []
    partner_totals = []
    for stride in range(1, STEPS + 1):
        partner, partner_total = from_behind((partner, partner_total), "wide", 1)
        partner_totals.append(partner_total)
        rest = lax.map(
            lambda layer: jnp.sum(jnp.minimum(layer[:, None, :], partner[None, :, :]), axis=-1),
            jnp.transpose(high, (1, 0, 2)),
        )
        numerator = low_sum[:, :, None] + jnp.transpose(rest, (1, 0, 2))
        numerators.append(numerator.reshape(row_count, pivot_count * row_count))
    stacked = jnp.stack(numerators, axis=1)
    shares = lax.psum_scatter(stacked, "fields", scatter_dimension=2, tiled=True)
    share_width = shares.shape[2]
    offset = lax.axis_index("fields") * share_width
    step_totals = jnp.stack(partner_totals, axis=0)
    denominator = (
        owned_total[:, None, None, None]
        + pivot_total[None, None, :, None]
        + step_totals[None, :, None, :]
    )
    denominator = denominator.reshape(row_count, STEPS, pivot_count * row_count)
    denominator = lax.dynamic_slice_in_dim(denominator, offset, share_width, 2)
    return 1.5 * shares / denominator


def kernel(n_wide, n_fields, ids_ref, v_ref, out_ref, part, contrib, given, piv, pb, near, acc, low,
           own_sum, part_sum, msg, got, load_sem, c_send, c_recv, p_send, p_recv, b_send, b_recv,
           r_send, r_recv):
    rows = v_ref.shape[0]
    pivots = piv.shape[1]
    width = part.shape[3]
    cols = width // LANES
    share = pivots // n_fields
    me = lax.axis_index("wide")
    field = lax.axis_index("fields")
    parity = lax.rem(me, 2)
    beside = me + 1 - 2 * parity
    ahead = lax.rem(me + 2, n_wide)

    def wide_peer(d):
        return {"wide": lax.rem(me + d, n_wide)}

    def field_peer(d):
        return {"fields": lax.rem(field + d, n_fields)}

    for i in range(n_wide):
        pltpu.make_async_copy(
            v_ref.at[:, pl.ds(i * width, width)], part.at[i, 0], load_sem.at[i]
        ).start()

    barrier = pltpu.get_barrier_semaphore()
    for d in range(1, n_wide):
        pl.semaphore_signal(barrier, inc=1, device_id=wide_peer(d), device_id_type=MESH)
    for d in range(1, n_fields):
        pl.semaphore_signal(barrier, inc=1, device_id=field_peer(d), device_id_type=MESH)

    for q in range(pivots):
        row = ids_ref[q] - me * rows
        inside = jnp.logical_and(row >= 0, row < rows)
        values = v_ref[pl.ds(jnp.where(inside, row, 0), 1), :]
        values = jnp.where(inside, values, 0.0)
        for i in range(n_wide):
            contrib[i, q : q + 1, :] = values[:, i * width : (i + 1) * width]
    for i in range(n_wide):
        pltpu.make_async_copy(
            v_ref.at[:, pl.ds(i * width, width)], part.at[i, 0], load_sem.at[i]
        ).wait()
    pl.semaphore_wait(barrier, n_wide - 1 + n_fields - 1)

    def c_copy(d):
        return pltpu.make_async_remote_copy(
            src_ref=contrib.at[lax.rem(me + d, n_wide)], dst_ref=given.at[d],
            send_sem=c_send.at[d], recv_sem=c_recv.at[d],
            device_id=wide_peer(d), device_id_type=MESH)

    def p_copy(d):
        return pltpu.make_async_remote_copy(
            src_ref=piv.at[me], dst_ref=piv.at[me],
            send_sem=p_send.at[d], recv_sem=p_recv.at[d],
            device_id=wide_peer(d), device_id_type=MESH)

    def b_copy(kind, i, source, slot, target):
        return pltpu.make_async_remote_copy(
            src_ref=part.at[i, source], dst_ref=part.at[i, slot],
            send_sem=b_send.at[kind, i], recv_sem=b_recv.at[kind, i],
            device_id={"wide": target}, device_id_type=MESH)

    def hop_ahead(i):
        return b_copy(0, i, 0, 2, ahead)

    def relay_ahead(i):
        return b_copy(1, i, 2, 4, ahead)

    def first_beside(i):
        return b_copy(2, i, 2 * parity, 1, beside)

    def second_beside(i):
        return b_copy(3, i, 2 + 2 * parity, 3, beside)

    def stage0(i):
        hop_ahead(i).start()

        @pl.when(parity == 0)
        def _():
            first_beside(i).start()

    def stage1(i):
        hop_ahead(i).wait_recv()
        relay_ahead(i).start()

        @pl.when(parity == 1)
        def _():
            first_beside(i).start()

        @pl.when(parity == 0)
        def _():
            second_beside(i).start()

    def stage2(i):
        relay_ahead(i).wait_recv()

        @pl.when(parity == 1)
        def _():
            second_beside(i).start()

    for d in range(1, n_wide):
        c_copy(d).start()
    stage0(0)
    stage0(1)
    acc[...] = jnp.zeros_like(acc)
    low[...] = jnp.zeros_like(low)
    own_sum[...] = jnp.zeros_like(own_sum)
    part_sum[...] = jnp.zeros_like(part_sum)
    for d in range(1, n_wide):
        c_copy(d).wait_recv()
    total = contrib[me]
    for d in range(1, n_wide):
        total = total + given[d]
    piv[me] = total
    for d in range(1, n_wide):
        p_copy(d).start()
    stage1(0)
    stage0(2)
    stage1(1)
    stage2(0)
    for d in range(1, n_wide):
        source = lax.rem(me + n_wide - d, n_wide)
        pltpu.make_async_remote_copy(
            src_ref=piv.at[source], dst_ref=piv.at[source],
            send_sem=p_send.at[d], recv_sem=p_recv.at[d],
            device_id=wide_peer(d), device_id_type=MESH).wait_recv()

    place = lax.broadcasted_iota(jnp.int32, (1, LANES), 1) * n_fields + field
    scale = jnp.exp2(place.astype(jnp.float32) / (LANES * n_fields))
    unscale = 1.0 / scale

    def prepare(i, half):
        for k in range(cols):
            lane = slice(k * LANES, (k + 1) * LANES)
            to = slice(half * width + k * LANES, half * width + (k + 1) * LANES)
            own_sum[...] += part[i, 0, :, lane]
            for s in range(STEPS):
                other = part[i, s + 1, :, lane]
                part_sum[s] += other
                near[s * rows : (s + 1) * rows, to] = (other * scale).astype(jnp.bfloat16)
        for q in range(pivots):
            line = piv[i, q : q + 1, :] * jnp.concatenate([scale] * cols, axis=1)
            spread = jnp.broadcast_to(line, (PACK, width)).astype(jnp.bfloat16)
            pb[q, :, half * width : (half + 1) * width] = spread

    def step(t, carry):
        i = 2 * t

        @pl.when(i + 3 < n_wide)
        def _():
            stage0(i + 3)

        @pl.when(i + 2 < n_wide)
        def _():
            stage1(i + 2)

        stage2(i + 1)

        @pl.when(i + 4 < n_wide)
        def _():
            stage0(i + 4)

        first_beside(i).wait_recv()
        second_beside(i).wait_recv()
        prepare(i, 0)

        @pl.when(i + 3 < n_wide)
        def _():
            stage1(i + 3)

        @pl.when(i + 2 < n_wide)
        def _():
            stage2(i + 2)

        first_beside(i + 1).wait_recv()
        second_beside(i + 1).wait_recv()
        prepare(i + 1, 1)

        def per_row(v, inner):
            at = pl.ds(pl.multiple_of(i * width, LANES), 2 * width)
            own = v_ref[pl.ds(v, 1), at]
            low_now = None
            mine = []
            for k in range(2 * cols):
                line = own[:, k * LANES : (k + 1) * LANES]
                wide_line = jnp.broadcast_to(line * scale, (PACK, LANES))
                mine.append(wide_line.astype(jnp.bfloat16))
                c = k % cols
                small = jnp.minimum(line, piv[i + k // cols, :, c * LANES : (c + 1) * LANES])
                low_now = small if low_now is None else low_now + small
            low[v] += low_now
            for q0 in range(0, pivots, QGROUP):
                high = [
                    jnp.maximum(mine[k][None], pb[q0 : q0 + QGROUP, :, k * LANES : (k + 1) * LANES])
                    for k in range(2 * cols)
                ]
                for g in range(STEPS * rows // PACK):
                    line = slice(g * PACK, (g + 1) * PACK)
                    terms = [
                        jnp.minimum(high[k], near[line, k * LANES : (k + 1) * LANES][None])
                        for k in range(2 * cols)
                    ]
                    while len(terms) > 1:
                        terms = [
                            terms[j] + terms[j + 1] if j + 1 < len(terms) else terms[j]
                            for j in range(0, len(terms), 2)
                        ]
                    acc[v, q0 : q0 + QGROUP, line, :] += terms[0].astype(jnp.float32)
            return inner

        lax.fori_loop(0, rows, per_row, 0)
        return carry

    lax.fori_loop(0, n_wide // 2, step, 0)

    lane_at = lax.broadcasted_iota(jnp.int32, (SUB, LANES), 1)
    sub_at = lax.broadcasted_iota(jnp.int32, (SUB, LANES), 0)

    def finish(v, inner):
        low_sum = jnp.sum(low[v], axis=-1, keepdims=True)
        for q in range(pivots):
            spread = jnp.zeros((SUB, LANES), jnp.float32)
            for g in range(LANES // SUB):
                piece = acc[v, q, g * SUB : (g + 1) * SUB, :] * unscale
                piece = jnp.sum(piece, axis=-1, keepdims=True)
                spread = jnp.where(lane_at // SUB == g, piece, spread)
            spread = jnp.where(lane_at % SUB == sub_at, spread, 0.0)
            line = jnp.sum(spread, axis=0, keepdims=True) + low_sum[q : q + 1]
            msg[q // share, pl.ds(q % share * rows + v, 1), :] = line
        return inner

    lax.fori_loop(0, rows, finish, 0)
    own_total = jnp.sum(own_sum[...], axis=-1, keepdims=True)
    part_total = jnp.sum(part_sum[...].reshape(STEPS * rows, LANES).T, axis=0, keepdims=True)
    pivot_total = jnp.sum(jnp.sum(piv[...], axis=0), axis=-1, keepdims=True)
    pivot_total = jnp.broadcast_to(pivot_total, (pivots, LANES))
    base = own_total + part_total
    for j in range(n_fields):
        msg[j, share * rows : (share + 1) * rows, :] = base
        at = (share + 1) * rows
        for q in range(pivots):
            turned = (j * share + q) % pivots
            msg[j, at + q : at + q + 1, :] = pivot_total[turned : turned + 1]

    def r_copy(d):
        return pltpu.make_async_remote_copy(
            src_ref=msg.at[lax.rem(field + d, n_fields)], dst_ref=got.at[d],
            send_sem=r_send.at[d], recv_sem=r_recv.at[d],
            device_id=field_peer(d), device_id_type=MESH)

    for d in range(1, n_fields):
        r_copy(d).start()
    for d in range(1, n_fields):
        r_copy(d).wait_recv()
    whole = msg[field]
    for d in range(1, n_fields):
        whole = whole + got[d]
    base = whole[share * rows : (share + 1) * rows]
    at = (share + 1) * rows
    for q in range(share):
        denominator = base + whole[at + q : at + q + 1]
        out_ref[q] = 1.5 * whole[q * rows : (q + 1) * rows] / denominator

    for d in range(1, n_wide):
        c_copy(d).wait_send()
        p_copy(d).wait_send()
    for i in range(n_wide):
        hop_ahead(i).wait_send()
        relay_ahead(i).wait_send()
        first_beside(i).wait_send()
        second_beside(i).wait_send()
    for d in range(1, n_fields):
        r_copy(d).wait_send()


def fused_body(vectors, pivot_ids, n_wide, n_fields):
    rows, local = vectors.shape
    pivots = pivot_ids.shape[0]
    width = local // n_wide
    share = pivots // n_fields
    f32 = jnp.float32
    dma = pltpu.SemaphoreType.DMA
    lines = (share + 1) * rows + pivots
    table = pl.pallas_call(
        functools.partial(kernel, n_wide, n_fields),
        out_shape=jax.ShapeDtypeStruct((share, rows, STEPS * rows), f32),
        in_specs=[
            pl.BlockSpec(memory_space=pltpu.SMEM),
            pl.BlockSpec(memory_space=pltpu.VMEM),
        ],
        out_specs=pl.BlockSpec(memory_space=pltpu.VMEM),
        scratch_shapes=[
            pltpu.VMEM((n_wide, STEPS + 1, rows, width), f32),
            pltpu.VMEM((n_wide, pivots, width), f32),
            pltpu.VMEM((n_wide, pivots, width), f32),
            pltpu.VMEM((n_wide, pivots, width), f32),
            pltpu.VMEM((pivots, PACK, 2 * width), jnp.bfloat16),
            pltpu.VMEM((STEPS * rows, 2 * width), jnp.bfloat16),
            pltpu.VMEM((rows, pivots, STEPS * rows, LANES), f32),
            pltpu.VMEM((rows, pivots, LANES), f32),
            pltpu.VMEM((rows, LANES), f32),
            pltpu.VMEM((STEPS, rows, LANES), f32),
            pltpu.VMEM((n_fields, lines, LANES), f32),
            pltpu.VMEM((n_fields, lines, LANES), f32),
            dma((n_wide,)),
            dma((n_wide,)), dma((n_wide,)),
            dma((n_wide,)), dma((n_wide,)),
            dma((4, n_wide)), dma((4, n_wide)),
            dma((n_fields,)), dma((n_fields,)),
        ],
        compiler_params=pltpu.CompilerParams(
            collective_id=0, has_side_effects=True, vmem_limit_bytes=48 * 1024 * 1024
        ),
    )(pivot_ids, vectors)
    table = table.reshape(share, rows, STEPS, rows)
    return jnp.transpose(table, (1, 2, 0, 3)).reshape(rows, STEPS, share * rows)


def solution(mesh):
    n_wide = mesh.shape["wide"]
    n_fields = mesh.shape["fields"]

    def body(vectors, pivot_ids):
        rows, local = vectors.shape
        pivots = pivot_ids.shape[0]
        fits = (
            n_wide % 2 == 0 and n_wide > STEPS and local % (n_wide * LANES) == 0
            and pivots % n_fields == 0 and pivots == SUB and rows % SUB == 0
            and STEPS * rows == LANES
        )
        if fits:
            return fused_body(vectors, pivot_ids, n_wide, n_fields)
        return plain_body(vectors, pivot_ids)

    placed = (P("wide", "fields"), P())
    return jax.shard_map(
        body, mesh=mesh, in_specs=placed, out_specs=P("wide", None, "fields"), check_vma=False
    )
```

```python
import functools

import jax
import jax.numpy as jnp
from jax import lax
from jax.experimental import pallas as pl
from jax.experimental.pallas import tpu as pltpu
from jax.sharding import PartitionSpec as P

STEPS = 4
LANES = 128
SUB = 8
PACK = 16
QGROUP = 4
MESH = pl.DeviceIdType.MESH


def from_behind(value, axis, steps):
    count = lax.axis_size(axis)
    pairs = [(source, (source + steps) % count) for source in range(count)]
    return lax.ppermute(value, axis, pairs)


def plain_body(vectors, pivot_ids):
    row_count = vectors.shape[0]
    pivot_count = pivot_ids.shape[0]
    first_row = lax.axis_index("wide") * row_count
    chosen = (
        pivot_ids[:, None] == first_row + jnp.arange(row_count, dtype=jnp.int32)[None, :]
    ).astype(jnp.float32)
    pivot_part = jnp.dot(
        chosen, vectors, precision=lax.Precision.HIGHEST, preferred_element_type=jnp.float32
    )
    pivots = lax.psum(pivot_part, "wide")
    owned_total, pivot_total = lax.psum(
        (jnp.sum(vectors, axis=1), jnp.sum(pivots, axis=1)), "fields"
    )
    low = jnp.minimum(vectors[:, None, :], pivots[None, :, :])
    high = jnp.maximum(vectors[:, None, :], pivots[None, :, :])
    low_sum = jnp.sum(low, axis=-1)
    partner, partner_total = (vectors, owned_total)
    numerators = []
    partner_totals = []
    for stride in range(1, STEPS + 1):
        partner, partner_total = from_behind((partner, partner_total), "wide", 1)
        partner_totals.append(partner_total)
        rest = lax.map(
            lambda layer: jnp.sum(jnp.minimum(layer[:, None, :], partner[None, :, :]), axis=-1),
            jnp.transpose(high, (1, 0, 2)),
        )
        numerator = low_sum[:, :, None] + jnp.transpose(rest, (1, 0, 2))
        numerators.append(numerator.reshape(row_count, pivot_count * row_count))
    stacked = jnp.stack(numerators, axis=1)
    shares = lax.psum_scatter(stacked, "fields", scatter_dimension=2, tiled=True)
    share_width = shares.shape[2]
    offset = lax.axis_index("fields") * share_width
    step_totals = jnp.stack(partner_totals, axis=0)
    denominator = (
        owned_total[:, None, None, None]
        + pivot_total[None, None, :, None]
        + step_totals[None, :, None, :]
    )
    denominator = denominator.reshape(row_count, STEPS, pivot_count * row_count)
    denominator = lax.dynamic_slice_in_dim(denominator, offset, share_width, 2)
    return 1.5 * shares / denominator


def kernel(n_wide, n_fields, ids_ref, v_ref, out_ref, part, contrib, given, piv, pb, near, acc, low,
           own_sum, part_sum, msg, got, load_sem, c_send, c_recv, p_send, p_recv, b_send, b_recv,
           r_send, r_recv):
    rows = v_ref.shape[0]
    pivots = piv.shape[1]
    width = part.shape[3]
    cols = width // LANES
    share = pivots // n_fields
    me = lax.axis_index("wide")
    field = lax.axis_index("fields")
    parity = lax.rem(me, 2)
    beside = me + 1 - 2 * parity
    ahead = lax.rem(me + 2, n_wide)
    back = lax.rem(me + n_wide - 2, n_wide)

    def wide_peer(d):
        return {"wide": lax.rem(me + d, n_wide)}

    def field_peer(d):
        return {"fields": lax.rem(field + d, n_fields)}

    for i in range(n_wide):
        pltpu.make_async_copy(
            v_ref.at[:, pl.ds(i * width, width)], part.at[i, 0], load_sem.at[i]
        ).start()

    barrier = pltpu.get_barrier_semaphore()
    for d in range(1, n_wide):
        pl.semaphore_signal(barrier, inc=1, device_id=wide_peer(d), device_id_type=MESH)
    for d in range(1, n_fields):
        pl.semaphore_signal(barrier, inc=1, device_id=field_peer(d), device_id_type=MESH)

    for q in range(pivots):
        row = ids_ref[q] - me * rows
        inside = jnp.logical_and(row >= 0, row < rows)
        values = v_ref[pl.ds(jnp.where(inside, row, 0), 1), :]
        values = jnp.where(inside, values, 0.0)
        for i in range(n_wide):
            contrib[i, q : q + 1, :] = values[:, i * width : (i + 1) * width]
    for i in range(n_wide):
        pltpu.make_async_copy(
            v_ref.at[:, pl.ds(i * width, width)], part.at[i, 0], load_sem.at[i]
        ).wait()
    pl.semaphore_wait(barrier, n_wide - 1 + n_fields - 1)

    def c_copy(d):
        return pltpu.make_async_remote_copy(
            src_ref=contrib.at[lax.rem(me + d, n_wide)], dst_ref=given.at[d],
            send_sem=c_send.at[d], recv_sem=c_recv.at[d],
            device_id=wide_peer(d), device_id_type=MESH)

    def p_copy(d):
        return pltpu.make_async_remote_copy(
            src_ref=piv.at[me], dst_ref=piv.at[me],
            send_sem=p_send.at[d], recv_sem=p_recv.at[d],
            device_id=wide_peer(d), device_id_type=MESH)

    def b_copy(kind, i, source, slot, target):
        return pltpu.make_async_remote_copy(
            src_ref=part.at[i, source], dst_ref=part.at[i, slot],
            send_sem=b_send.at[kind, i], recv_sem=b_recv.at[kind, i],
            device_id={"wide": target}, device_id_type=MESH)

    def route(i):
        return True, False

    def hop_ahead(i):
        return b_copy(0, i, 0, 2, ahead)

    def hop_back(i):
        return b_copy(4, i, 0, 5, back)

    def relay(i):
        forward, _ = route(i)
        return b_copy(1, i, 2, 4, ahead) if forward else b_copy(1, i, 5, 4, back)

    def first_beside(i):
        return b_copy(2, i, 2 * parity, 1, beside)

    def third(i):
        _, along = route(i)
        return b_copy(3, i, 1, 3, ahead) if along else b_copy(3, i, 2 + 2 * parity, 3, beside)

    def stage0(i):
        forward, _ = route(i)
        hop_ahead(i).start()
        if not forward:
            hop_back(i).start()

        @pl.when(parity == 0)
        def _():
            first_beside(i).start()

    def stage1(i):
        forward, along = route(i)
        hop_ahead(i).wait_recv()
        if forward:
            relay(i).start()

        @pl.when(parity == 1)
        def _():
            first_beside(i).start()

        if not along:
            @pl.when(parity == 0)
            def _():
                third(i).start()

        if not forward:
            hop_back(i).wait_recv()
            relay(i).start()

    def stage2(i):
        _, along = route(i)
        if along:
            first_beside(i).wait_recv()
            third(i).start()
            relay(i).wait_recv()
        else:
            relay(i).wait_recv()

            @pl.when(parity == 1)
            def _():
                third(i).start()

            first_beside(i).wait_recv()

    for d in range(1, n_wide):
        c_copy(d).start()
    stage0(0)
    stage0(1)
    stage0(2)
    acc[...] = jnp.zeros_like(acc)
    low[...] = jnp.zeros_like(low)
    own_sum[...] = jnp.zeros_like(own_sum)
    part_sum[...] = jnp.zeros_like(part_sum)
    for d in range(1, n_wide):
        c_copy(d).wait_recv()
    total = contrib[me]
    for d in range(1, n_wide):
        total = total + given[d]
    piv[me] = total
    for d in range(1, n_wide):
        p_copy(d).start()
    for d in range(1, n_wide):
        source = lax.rem(me + n_wide - d, n_wide)
        pltpu.make_async_remote_copy(
            src_ref=piv.at[source], dst_ref=piv.at[source],
            send_sem=p_send.at[d], recv_sem=p_recv.at[d],
            device_id=wide_peer(d), device_id_type=MESH).wait_recv()

    place = lax.broadcasted_iota(jnp.int32, (1, LANES), 1) * n_fields + field
    scale = jnp.exp2(place.astype(jnp.float32) / (LANES * n_fields))
    unscale = 1.0 / scale

    def prepare(i, half):
        for k in range(cols):
            lane = slice(k * LANES, (k + 1) * LANES)
            to = slice(half * width + k * LANES, half * width + (k + 1) * LANES)
            own_sum[...] += part[i, 0, :, lane]
            for s in range(STEPS):
                other = part[i, s + 1, :, lane]
                part_sum[s] += other
                near[s * rows : (s + 1) * rows, to] = (other * scale).astype(jnp.bfloat16)
        for q in range(pivots):
            line = piv[i, q : q + 1, :] * jnp.concatenate([scale] * cols, axis=1)
            spread = jnp.broadcast_to(line, (PACK, width)).astype(jnp.bfloat16)
            pb[q, :, half * width : (half + 1) * width] = spread

    stages = (stage0, stage1, stage2)
    lead = [(1, 0), (0, 3), (1, 1), (2, 0), (0, 4), (1, 2), (2, 1)]
    points = []
    for i in range(2, n_wide, 2):
        points.append([[(1, i + 1), (0, i + 3)], [(2, i)], [(1, i + 2), (0, i + 4)], [(2, i + 1)]])

    def issue(pairs):
        for kind, i in pairs:
            if i < n_wide:
                stages[kind](i)

    issue(lead)

    def step(t):
        i = 2 * t
        third(i).wait_recv()
        prepare(i, 0)
        third(i + 1).wait_recv()
        prepare(i + 1, 1)

        def per_row(v, inner):
            at = pl.ds(i * width, 2 * width)
            own = v_ref[pl.ds(v, 1), at]
            low_now = None
            mine = []
            for k in range(2 * cols):
                line = own[:, k * LANES : (k + 1) * LANES]
                wide_line = jnp.broadcast_to(line * scale, (PACK, LANES))
                mine.append(wide_line.astype(jnp.bfloat16))
                c = k % cols
                small = jnp.minimum(line, piv[i + k // cols, :, c * LANES : (c + 1) * LANES])
                low_now = small if low_now is None else low_now + small
            low[v] += low_now
            for q0 in range(0, pivots, QGROUP):
                high = [
                    jnp.maximum(mine[k][None], pb[q0 : q0 + QGROUP, :, k * LANES : (k + 1) * LANES])
                    for k in range(2 * cols)
                ]
                for g in range(STEPS * rows // PACK):
                    line = slice(g * PACK, (g + 1) * PACK)
                    terms = [
                        jnp.minimum(high[k], near[line, k * LANES : (k + 1) * LANES][None])
                        for k in range(2 * cols)
                    ]
                    while len(terms) > 1:
                        terms = [
                            terms[j] + terms[j + 1] if j + 1 < len(terms) else terms[j]
                            for j in range(0, len(terms), 2)
                        ]
                    acc[v, q0 : q0 + QGROUP, line, :] += terms[0].astype(jnp.float32)
            return inner

        todo = points[t] if t < len(points) else []
        if not todo:
            lax.fori_loop(0, rows, per_row, 0)
        for j, pairs in enumerate(todo):
            issue(pairs)
            lax.fori_loop(j * rows // len(todo), (j + 1) * rows // len(todo), per_row, 0)

    for t in range(n_wide // 2):
        step(t)

    lane_at = lax.broadcasted_iota(jnp.int32, (SUB, LANES), 1)
    sub_at = lax.broadcasted_iota(jnp.int32, (SUB, LANES), 0)

    def finish(v, inner):
        low_sum = jnp.sum(low[v], axis=-1, keepdims=True)
        for q in range(pivots):
            spread = jnp.zeros((SUB, LANES), jnp.float32)
            for g in range(LANES // SUB):
                piece = acc[v, q, g * SUB : (g + 1) * SUB, :] * unscale
                piece = jnp.sum(piece, axis=-1, keepdims=True)
                spread = jnp.where(lane_at // SUB == g, piece, spread)
            spread = jnp.where(lane_at % SUB == sub_at, spread, 0.0)
            line = jnp.sum(spread, axis=0, keepdims=True) + low_sum[q : q + 1]
            msg[q // share, pl.ds(q % share * rows + v, 1), :] = line
        return inner

    lax.fori_loop(0, rows, finish, 0)
    own_total = jnp.sum(own_sum[...], axis=-1, keepdims=True)
    part_total = jnp.sum(part_sum[...].reshape(STEPS * rows, LANES).T, axis=0, keepdims=True)
    pivot_total = jnp.sum(jnp.sum(piv[...], axis=0), axis=-1, keepdims=True)
    pivot_total = jnp.broadcast_to(pivot_total, (pivots, LANES))
    base = own_total + part_total
    for j in range(n_fields):
        msg[j, share * rows : (share + 1) * rows, :] = base
        at = (share + 1) * rows
        for q in range(pivots):
            turned = (j * share + q) % pivots
            msg[j, at + q : at + q + 1, :] = pivot_total[turned : turned + 1]

    def r_copy(d):
        return pltpu.make_async_remote_copy(
            src_ref=msg.at[lax.rem(field + d, n_fields)], dst_ref=got.at[d],
            send_sem=r_send.at[d], recv_sem=r_recv.at[d],
            device_id=field_peer(d), device_id_type=MESH)

    for d in range(1, n_fields):
        r_copy(d).start()
    for d in range(1, n_fields):
        r_copy(d).wait_recv()
    whole = msg[field]
    for d in range(1, n_fields):
        whole = whole + got[d]
    base = whole[share * rows : (share + 1) * rows]
    at = (share + 1) * rows
    for q in range(share):
        denominator = base + whole[at + q : at + q + 1]
        out_ref[q] = 1.5 * whole[q * rows : (q + 1) * rows] / denominator

    for d in range(1, n_wide):
        c_copy(d).wait_send()
        p_copy(d).wait_send()
    for i in range(n_wide):
        hop_ahead(i).wait_send()
        if not route(i)[0]:
            hop_back(i).wait_send()
        relay(i).wait_send()
        first_beside(i).wait_send()
        third(i).wait_send()
    for d in range(1, n_fields):
        r_copy(d).wait_send()


def fused_body(vectors, pivot_ids, n_wide, n_fields):
    rows, local = vectors.shape
    pivots = pivot_ids.shape[0]
    width = local // n_wide
    share = pivots // n_fields
    f32 = jnp.float32
    dma = pltpu.SemaphoreType.DMA
    lines = (share + 1) * rows + pivots
    table = pl.pallas_call(
        functools.partial(kernel, n_wide, n_fields),
        out_shape=jax.ShapeDtypeStruct((share, rows, STEPS * rows), f32),
        in_specs=[
            pl.BlockSpec(memory_space=pltpu.SMEM),
            pl.BlockSpec(memory_space=pltpu.VMEM),
        ],
        out_specs=pl.BlockSpec(memory_space=pltpu.VMEM),
        scratch_shapes=[
            pltpu.VMEM((n_wide, STEPS + 2, rows, width), f32),
            pltpu.VMEM((n_wide, pivots, width), f32),
            pltpu.VMEM((n_wide, pivots, width), f32),
            pltpu.VMEM((n_wide, pivots, width), f32),
            pltpu.VMEM((pivots, PACK, 2 * width), jnp.bfloat16),
            pltpu.VMEM((STEPS * rows, 2 * width), jnp.bfloat16),
            pltpu.VMEM((rows, pivots, STEPS * rows, LANES), f32),
            pltpu.VMEM((rows, pivots, LANES), f32),
            pltpu.VMEM((rows, LANES), f32),
            pltpu.VMEM((STEPS, rows, LANES), f32),
            pltpu.VMEM((n_fields, lines, LANES), f32),
            pltpu.VMEM((n_fields, lines, LANES), f32),
            dma((n_wide,)),
            dma((n_wide,)), dma((n_wide,)),
            dma((n_wide,)), dma((n_wide,)),
            dma((5, n_wide)), dma((5, n_wide)),
            dma((n_fields,)), dma((n_fields,)),
        ],
        compiler_params=pltpu.CompilerParams(
            collective_id=0, has_side_effects=True, vmem_limit_bytes=48 * 1024 * 1024
        ),
    )(pivot_ids, vectors)
    table = table.reshape(share, rows, STEPS, rows)
    return jnp.transpose(table, (1, 2, 0, 3)).reshape(rows, STEPS, share * rows)


def solution(mesh):
    n_wide = mesh.shape["wide"]
    n_fields = mesh.shape["fields"]

    def body(vectors, pivot_ids):
        rows, local = vectors.shape
        pivots = pivot_ids.shape[0]
        fits = (
            n_wide == 2 * STEPS and local % (n_wide * LANES) == 0
            and pivots % n_fields == 0 and pivots == SUB and rows % SUB == 0
            and STEPS * rows == LANES
        )
        if fits:
            return fused_body(vectors, pivot_ids, n_wide, n_fields)
        return plain_body(vectors, pivot_ids)

    placed = (P("wide", "fields"), P())
    return jax.shard_map(
        body, mesh=mesh, in_specs=placed, out_specs=P("wide", None, "fields"), check_vma=False
    )
```
